32 devices in a mesh: groups: 2 (over y), row: 4 (over x, core), col: 4 (over z).
Axes of the slice: x: 2, y: 2, z: 4, core: 2. Of those that a mesh axis runs over, the one named last changes fastest.
Arguments:
- tokens: bfloat16 [2048, 8192], P('groups', ('row', 'col')), parts along dimension 0, may hold values from -6 to 6
- gate_weight: bfloat16 [8192, 26624], P('row', 'col'), may hold values from -0.0625 to 0.0625
- up_weight: bfloat16 [8192, 26624], P('row', 'col'), may hold values from -0.0625 to 0.0625
- down_weight: bfloat16 [26624, 8192], P('col', 'row'), may hold values from -0.0546875 to 0.0546875
Outputs:
- mixed: bfloat16 [2048, 8192], P('groups', ('row', 'col')), parts along dimension 0
The draws below stay inside these ranges and needn't reach their ends.
There are 2 independent parts, one for each index of `groups`. The reference program is written for one: setup_inputs(seed, part) draws one part's arguments, and reference() takes and returns one part's arrays. A program takes and returns all parts, laid end to end along the dimension named above; an argument that names none is the same for every part. Nothing has to cross between parts.
All inputs are finite; a program needn't handle non-finite values.
Results may differ from the reference program's by a relative error of at most 0.02.
Values may be sent and summed in bfloat16 or wider, within the bound.
No kernel may reach another device: no remote copies, remote signals or barrier semaphores. Data moves between devices by JAX's collectives and lax.ppermute only.
A program may use at most 256 MiB of HBM per device.

```python
import jax
import jax.numpy as jnp
from jax import lax

D = 8192
FF = 26624
ROWS = 1024
N_ROW = 4
N_COL = 4


def raised(array, rng, source, target, parts, factor):
    owner, partner = [(jnp.arange(array.shape[dim]) // (array.shape[dim] // parts)).reshape([-1 if axis == dim else 1 for axis in range(array.ndim)]) for dim in (source, target)]
    chosen = jax.random.permutation(rng, parts)[partner]
    strong = (owner == chosen) | (owner == (partner + parts // 2) % parts)
    return jnp.where(strong, factor * array, array)


def level_of(own_key, extent, cuts, smallest, high):
    gain = 1.0
    for position, shards_of in cuts:
        draws = jax.random.uniform(jax.random.fold_in(jax.random.fold_in(own_key, 6), position), (shards_of,), jnp.float32, smallest / len(cuts), high / len(cuts))
        gain = gain * jnp.repeat(jnp.exp(draws), extent[position] // shards_of).reshape((-1,) + (1,) * (len(extent) - 1 - position))
    return gain


def centred(stream_key, dims, width, bound, shards=(), kind=jnp.bfloat16):
    gain = level_of(stream_key, dims, shards, -0.22, 0.18) if shards else 1.0
    result = jax.random.normal(stream_key, dims, jnp.float32) * width * gain
    return jnp.minimum(jnp.maximum(result, -bound), bound).astype(kind)


def bell_draw_with(rng, dims, spread, bound, pieces, heavy, kind=jnp.bfloat16):
    values = spread * jax.random.normal(rng, dims, jnp.float32)
    if pieces:
        values = values * level_of(rng, dims, pieces, -0.22, 0.18)
    return jnp.clip(raised(values, jax.random.fold_in(rng, 3), *heavy), -bound, bound).astype(kind)


def setup_inputs(seed: int = 0, part: int = 0) -> dict:
    key_of = jax.random.split(jax.random.key(seed), 5)
    own_keys = jax.random.split(jax.random.fold_in(key_of[4], part), 5)
    return {
        "tokens": bell_draw_with(own_keys[0], (ROWS, D), 1.0, 6.0, ((1, 16),), (1, 0, 16, 2.0)),
        "gate_weight": centred(key_of[1], (D, FF), D ** -0.5, 0.0625, ((0, 4), (1, 4))),
        "up_weight": centred(key_of[2], (D, FF), D ** -0.5, 0.0625, ((0, 4), (1, 4))),
        "down_weight": bell_draw_with(key_of[3], (FF, D), FF ** -0.5, 0.0546875, ((0, 4), (1, 4)), (0, 1, 4, 2.0)),
    }


def reference(tokens, gate_weight, up_weight, down_weight):
    feat_block = D // N_ROW
    hid_block = FF // N_COL

    def add_feature(carry, index):
        start = index * feat_block
        cols = lax.dynamic_slice_in_dim(tokens, start, feat_block, 1)
        gate_rows = lax.dynamic_slice_in_dim(gate_weight, start, feat_block, 0)
        up_rows = lax.dynamic_slice_in_dim(up_weight, start, feat_block, 0)
        gate_part = jnp.dot(cols, gate_rows, preferred_element_type=jnp.float32).astype(jnp.bfloat16)
        up_part = jnp.dot(cols, up_rows, preferred_element_type=jnp.float32).astype(jnp.bfloat16)
        return (carry[0] + gate_part.astype(jnp.float32), carry[1] + up_part.astype(jnp.float32)), None

    start_sums = (jnp.zeros((ROWS, FF), jnp.float32), jnp.zeros((ROWS, FF), jnp.float32))
    sums, unused = lax.scan(add_feature, start_sums, jnp.arange(N_ROW, dtype=jnp.int32))
    gate_sum, up_sum = sums
    hidden = (jax.nn.silu(gate_sum) * up_sum).astype(jnp.bfloat16)

    def add_hidden(carry, index):
        start = index * hid_block
        cols = lax.dynamic_slice_in_dim(hidden, start, hid_block, 1)
        rows = lax.dynamic_slice_in_dim(down_weight, start, hid_block, 0)
        part = jnp.dot(cols, rows, preferred_element_type=jnp.float32).astype(jnp.bfloat16)
        return carry + part.astype(jnp.float32), None

    total, unused_two = lax.scan(add_hidden, jnp.zeros((ROWS, D), jnp.float32), jnp.arange(N_COL, dtype=jnp.int32))
    return total.astype(jnp.bfloat16)
```

```python
import functools

import jax
import jax.numpy as jnp
import numpy as np
from jax import lax
from jax.experimental import pallas as pl
from jax.experimental.pallas import tpu as pltpu
from jax.sharding import PartitionSpec as P

BF16, F32 = jnp.bfloat16, jnp.float32
SCALE = 4
VMEM_LIMIT = 52 * 2**20
PARTNER, OWN, X, BLOCKS = 0, 1, 2, 3


def dot(a, b):
    return jnp.dot(a, b, preferred_element_type=F32)


def accumulate(tok_ref, gate_ref, up_ref, acc):
    step = pl.program_id(0)

    @pl.when(step == 0)
    def _():
        acc[0] = dot(tok_ref[...], gate_ref[...])
        acc[1] = dot(tok_ref[...], up_ref[...])

    @pl.when(step > 0)
    def _():
        acc[0] += dot(tok_ref[...], gate_ref[...])
        acc[1] += dot(tok_ref[...], up_ref[...])


def pieces_of(rows):
    half = rows // 2
    return [(which, start) for which in (0, 1) for start in (0, half)], half


def partner_kernel(place, tok_ref, gate_ref, up_ref, *rest):
    out_refs, acc = rest[:-1], rest[-1]
    accumulate(tok_ref, gate_ref, up_ref, acc)

    @pl.when(pl.program_id(0) == pl.num_programs(0) - 1)
    def _():
        pieces, height = pieces_of(acc.shape[1])
        for (which, start), out_ref in zip(pieces, out_refs):
            out_ref[...] = acc[which, start : start + height].astype(BF16)


def own_kernel(place, tok_ref, gate_ref, up_ref, *rest):
    received_refs, (send_ref, keep_ref, acc) = rest[:-3], rest[-3:]
    accumulate(tok_ref, gate_ref, up_ref, acc)
    half = send_ref.shape[1]

    @pl.when(pl.program_id(0) == pl.num_programs(0) - 1)
    def _():
        pieces, height = pieces_of(acc.shape[1])
        for (which, start), ref in zip(pieces, received_refs):
            acc[which, start : start + height] += ref[...].astype(F32)
        for ref, x in ((send_ref, 1 - place[X]), (keep_ref, place[X])):
            ref[...] = acc[:, pl.ds(pl.multiple_of(x * half, half), half), :].astype(BF16)


def down_kernel(place, own_x, other_x, own_x_core, other_x_core, weight_ref, *rest):
    out_refs, total = rest[:-1], rest[-1]
    step, part = pl.program_id(0), pl.program_id(1)

    def rows_of(mine, other):
        top = jnp.where(place[X] == 0, mine, other)
        bottom = jnp.where(place[X] == 0, other, mine)
        return jnp.concatenate([top, bottom], axis=0)

    @pl.when(part == 0)
    def _():
        total[...] = dot(rows_of(own_x[...], other_x[...]), weight_ref[...])

    @pl.when(part == 1)
    def _():
        value = total[...] + dot(rows_of(own_x_core[...], other_x_core[...]), weight_ref[...])
        if len(out_refs) == 1:
            out_refs[0][...] = value.astype(BF16)
            return
        for k, out_ref in enumerate(out_refs):
            @pl.when(step == k)
            def _(out_ref=out_ref):
                out_ref[...] = value.astype(BF16)


def whole(shape):
    return pl.BlockSpec(shape, lambda *_: (0,) * len(shape))


def params(n):
    return pltpu.CompilerParams(dimension_semantics=("arbitrary",) * n, vmem_limit_bytes=VMEM_LIMIT)


def cost(flops, *sizes):
    scale = SCALE
    return pl.CostEstimate(flops=int(flops * scale), bytes_accessed=int(sum(sizes) * scale), transcendentals=0)


def gate_up_call(place, tokens, rows, row_block, weights, n_col, which, span, received=None):
    part, of = span
    full, wide = weights[0].shape[0], weights[0].shape[1] // 2 // of
    depth, half = full // n_col, rows // 2
    weight = pl.BlockSpec((depth, wide), lambda k, place: (place[BLOCKS + k], place[which] * of + part))
    in_specs = [pl.BlockSpec((rows, depth), lambda k, place: (row_block, k)), weight, weight]
    operands = [tokens, *weights]
    if received is None:
        body, name = partner_kernel, "partner"
        out_shape, out_specs = [jax.ShapeDtypeStruct((half, wide), BF16)] * 4, [whole((half, wide))] * 4
    else:
        body, name = own_kernel, "own"
        out_shape, out_specs = [jax.ShapeDtypeStruct((2, half, wide), BF16)] * 2, [whole((2, half, wide))] * 2
        in_specs += [whole((half, wide))] * 4
        operands += received
    return pl.pallas_call(
        body,
        out_shape=out_shape,
        grid_spec=pltpu.PrefetchScalarGridSpec(
            num_scalar_prefetch=1,
            grid=(n_col,),
            in_specs=in_specs,
            out_specs=out_specs,
            scratch_shapes=[pltpu.VMEM((2, rows, wide), F32)],
        ),
        compiler_params=params(1),
        cost_estimate=cost(4 * rows * full * wide, 4 * full * wide, 4 * rows * wide),
        name=name,
    )(place, *operands)


def down_call(place, col, pieces, down_weight, n_col, split):
    half, wide = pieces[0].shape
    rows, block = 2 * half, down_weight.shape[1] // n_col
    if split:
        out_shape = [jax.ShapeDtypeStruct((rows, block), BF16)] * n_col
        out_specs = [whole((rows, block))] * n_col
        column = lambda d, place, col: lax.rem(col[0] + d + 1, n_col)
    else:
        out_shape = jax.ShapeDtypeStruct((rows, block * n_col), BF16)
        out_specs = pl.BlockSpec((rows, block), lambda d, k, place, col: (0, d))
        column = lambda d, place, col: d
    weight = pl.BlockSpec(
        (wide, block), lambda d, k, place, col: (jnp.where(k == 0, place[OWN], place[PARTNER]), column(d, place, col))
    )

    def body(place, col, *refs):
        down_kernel(place, *refs)

    return pl.pallas_call(
        body,
        out_shape=out_shape,
        grid_spec=pltpu.PrefetchScalarGridSpec(
            num_scalar_prefetch=2,
            grid=(n_col, 2),
            in_specs=[whole((half, wide))] * 4 + [weight],
            out_specs=out_specs,
            scratch_shapes=[pltpu.VMEM((rows, block), F32)],
        ),
        compiler_params=params(2),
        cost_estimate=cost(4 * rows * wide * block * n_col, 4 * wide * block * n_col, 8 * half * wide),
        name="down",
    )(place, col, *pieces, down_weight)


def shifted(x, n, shift):
    return lax.ppermute(x, "col", [(i, (i + shift) % n) for i in range(n)])


def swapped(x, mask):
    return lax.ppermute(x, "row", [(i, i ^ mask) for i in range(4)])


def after(x, *deps):
    return lax.optimization_barrier((x,) + deps)[0]


def pipelined(n_col, tokens, gate_weight, up_weight, down_weight):
    eighth = tokens.shape[0] // 8
    weights = (gate_weight, up_weight)
    row, col = lax.axis_index("row"), lax.axis_index("col")
    table = np.array(
        [
            [1 - r % 2, r % 2, r // 2] + [(c - s) % n_col for s in range(n_col)] + list(range(n_col)) + [c]
            for r in range(4)
            for c in range(n_col)
        ],
        np.int32,
    )
    mine = jnp.asarray(table)[row * n_col + col]
    by_shift, col_id = mine[: BLOCKS + n_col], mine[-1:]
    natural = jnp.concatenate([mine[:BLOCKS], mine[BLOCKS + n_col : -1]])

    def direct(piece):
        return [piece] + [shifted(piece, n_col, s) for s in range(1, n_col)]

    bounds = [0, 1, 3, 5, 7, 8]
    first = direct(tokens[:eighth])
    second = direct(after(tokens[eighth : 3 * eighth], *first[1:]))
    third = lax.all_gather(after(tokens[3 * eighth : 5 * eighth], *first[1:]), "col", axis=1, tiled=True)
    rest = lax.all_gather(after(tokens[5 * eighth :], third), "col", axis=1, tiled=True)
    sources = [
        (by_shift, jnp.concatenate(first, axis=1), 0),
        (by_shift, jnp.concatenate(second, axis=1), 0),
        (natural, third, 0),
        (natural, rest, 0),
        (natural, rest, 2),
    ]
    chunk_rows = [(b - a) * eighth for a, b in zip(bounds, bounds[1:])]
    last = [mine]

    def partner(i, span=(0, 1)):
        place, tok, block = sources[i]
        out = gate_up_call(after(place, *last), tok, chunk_rows[i], block, weights, n_col, PARTNER, span)
        last[:] = list(out)
        return [swapped(piece, 1) for piece in out]

    def own(i, received, span=(0, 1)):
        place, tok, block = sources[i]
        send, keep = gate_up_call(after(place, *last), tok, chunk_rows[i], block, weights, n_col, OWN, span, received)
        last[:] = [send]
        return keep, swapped(send, 2)

    def gated(pair):
        keep, arrived = after(pair[0], *last), pair[1]
        gate = keep[0].astype(F32) + arrived[0].astype(F32)
        up = keep[1].astype(F32) + arrived[1].astype(F32)
        hidden = (jax.nn.silu(gate) * up).astype(BF16)
        last[:] = [hidden]
        hidden_x = swapped(hidden, 2)
        return hidden, hidden_x, swapped(hidden, 1), swapped(hidden_x, 1)

    def down(pieces, split=False):
        out = down_call(after(by_shift, *last), col_id, pieces, down_weight, n_col, split)
        last[:] = list(out) if split else [out]
        if not split:
            return lax.psum_scatter(out, "col", scatter_dimension=1, tiled=True)
        total = out[-1].astype(F32)
        for s in range(1, n_col):
            total = total + shifted(out[s - 1], n_col, s).astype(F32)
        return total.astype(BF16)

    r0 = partner(0)
    p0 = own(0, r0)
    r1 = partner(1)
    h0 = gated(p0)
    p1 = own(1, r1)
    r2 = partner(2)
    o0 = down(h0)
    p2 = own(2, r2)
    h1 = gated(p1)
    r3 = partner(3)
    p3 = own(3, r3)
    o1 = down(h1)
    r4 = partner(4)
    h2 = gated(p2)
    p4 = own(4, r4)
    o2 = down(h2)
    h3 = gated(p3)
    h4 = gated(p4)
    o3 = down(h3)
    o4 = down(h4, split=True)
    return jnp.concatenate([o0, o1, o2, o3, o4], axis=0)


def generic(tokens, gate_weight, up_weight, down_weight):
    gathered = lax.all_gather(tokens, "col", axis=1, tiled=True)
    gate = lax.psum_scatter(dot(gathered, gate_weight).astype(BF16), "row", scatter_dimension=0, tiled=True)
    up = lax.psum_scatter(dot(gathered, up_weight).astype(BF16), "row", scatter_dimension=0, tiled=True)
    hidden = (jax.nn.silu(gate.astype(F32)) * up.astype(F32)).astype(BF16)
    hidden = lax.all_gather(hidden, "row", axis=0, tiled=True)
    partial = dot(hidden, down_weight).astype(BF16)
    return lax.psum_scatter(partial, "col", scatter_dimension=1, tiled=True)


def solution(mesh):
    n_row, n_col = mesh.shape["row"], mesh.shape["col"]
    in_specs = (P("groups", ("row", "col")), P("row", "col"), P("row", "col"), P("col", "row"))
    out_specs = P("groups", ("row", "col"))
    step = functools.partial(pipelined, n_col) if n_row == 4 else generic
    return jax.shard_map(step, mesh=mesh, in_specs=in_specs, out_specs=out_specs, check_vma=False)
```

```python
import functools

import jax
import jax.numpy as jnp
import numpy as np
from jax import lax
from jax.experimental import pallas as pl
from jax.experimental.pallas import tpu as pltpu
from jax.sharding import PartitionSpec as P

BF16, F32 = jnp.bfloat16, jnp.float32
GATE_UP_COST, DOWN_COST = 0.3, 4
SPLIT = (0, 1)
VMEM_LIMIT = 32 * 2**20
PARTNER, OWN, X, BLOCKS = 0, 1, 2, 3


def dot(a, b):
    return jnp.dot(a, b, preferred_element_type=F32)


def accumulate(place, token_refs, gate_ref, up_ref, stage, acc):
    step, depth = pl.program_id(0), gate_ref.shape[0]

    @pl.when(step == 0)
    def _():
        acc[...] = jnp.zeros_like(acc)
        for k in range(stage.shape[0]):
            if len(token_refs) == 1:
                stage[k] = token_refs[0][:, k * depth : (k + 1) * depth]
            else:
                stage[k] = token_refs[k][...]

    tok = stage[step]
    acc[0] += dot(tok, gate_ref[...])
    acc[1] += dot(tok, up_ref[...])


def pieces_of(rows, split):
    half = rows // 2
    if not split:
        return [(slice(0, 2), slice(0, rows))]
    return [(slice(w, w + 1), slice(at, at + half)) for w in (0, 1) for at in (0, half)]


def partner_kernel(n_tok, split, place, *refs):
    token_refs, (gate_ref, up_ref, *out_refs), (stage, acc) = refs[:n_tok], refs[n_tok:-2], refs[-2:]
    accumulate(place, token_refs, gate_ref, up_ref, stage, acc)

    @pl.when(pl.program_id(0) == pl.num_programs(0) - 1)
    def _():
        for (which, rows), out_ref in zip(pieces_of(acc.shape[1], split), out_refs):
            out_ref[...] = acc[which, rows].astype(BF16)


def own_kernel(n_tok, split, place, *refs):
    token_refs, (gate_ref, up_ref, *received_refs) = refs[:n_tok], refs[n_tok:-4]
    send_ref, keep_ref, stage, acc = refs[-4:]
    accumulate(place, token_refs, gate_ref, up_ref, stage, acc)
    half = send_ref.shape[1]

    @pl.when(pl.program_id(0) == pl.num_programs(0) - 1)
    def _():
        for (which, rows), ref in zip(pieces_of(acc.shape[1], split), received_refs):
            acc[which, rows] += ref[...].astype(F32)
        for ref, x in ((send_ref, 1 - place[X]), (keep_ref, place[X])):
            ref[...] = acc[:, pl.ds(pl.multiple_of(x * half, half), half), :].astype(BF16)


def down_kernel(n_col, split, place, col, own_x, other_x, own_x_core, other_x_core, weight_ref, *rest):
    out_refs, (own_half, partner_half) = rest[:-2], rest[-2:]
    step = pl.program_id(0)
    height, wide = own_x.shape

    @pl.when(step == 0)
    def _():
        for target, mine, other in ((own_half, own_x, other_x), (partner_half, own_x_core, other_x_core)):
            target[pl.ds(pl.multiple_of(place[X] * height, height), height), :] = mine[...]
            target[pl.ds(pl.multiple_of((1 - place[X]) * height, height), height), :] = other[...]

    block = weight_ref.shape[1] // n_col
    at = lax.rem(col[0] + step + 1, n_col) if split else step
    columns = pl.ds(pl.multiple_of(at * block, block), block)
    total = dot(own_half[...], weight_ref[pl.ds(pl.multiple_of(place[OWN] * wide, wide), wide), columns])
    total += dot(partner_half[...], weight_ref[pl.ds(pl.multiple_of(place[PARTNER] * wide, wide), wide), columns])
    value = total.astype(BF16)
    if not split:
        out_refs[0][...] = value
        return
    for k, out_ref in enumerate(out_refs):
        @pl.when(step == k)
        def _(out_ref=out_ref):
            out_ref[...] = value


def whole(shape):
    return pl.BlockSpec(shape, lambda *_: (0,) * len(shape), pipeline_mode=pl.Buffered(1))


def params(n):
    return pltpu.CompilerParams(dimension_semantics=("arbitrary",) * n, vmem_limit_bytes=VMEM_LIMIT)


def cost(scale, flops, *sizes):
    return pl.CostEstimate(flops=int(flops * scale), bytes_accessed=int(sum(sizes) * scale), transcendentals=0)


def gate_up_call(place, tokens, rows, row_block, weights, n_col, which, split, received=None):
    full, wide = weights[0].shape[0], weights[0].shape[1] // 2
    depth, half = full // n_col, rows // 2
    weight = pl.BlockSpec((depth, wide), lambda k, place: (place[BLOCKS + k], place[which]))
    token = pl.BlockSpec(
        (rows, tokens[0].shape[1]), lambda k, place: (row_block, 0), pipeline_mode=pl.Buffered(1)
    )
    in_specs = [token] * len(tokens) + [weight, weight]
    operands = [*tokens, *weights]
    shapes = [(w.stop - w.start, r.stop - r.start, wide) for w, r in pieces_of(rows, split)]
    if received is None:
        body, name = partner_kernel, "partner"
        out_shape, out_specs = [jax.ShapeDtypeStruct(a, BF16) for a in shapes], [whole(a) for a in shapes]
    else:
        body, name = own_kernel, "own"
        out_shape, out_specs = [jax.ShapeDtypeStruct((2, half, wide), BF16)] * 2, [whole((2, half, wide))] * 2
        in_specs += [whole(a) for a in shapes]
        operands += received
    return pl.pallas_call(
        functools.partial(body, len(tokens), split),
        out_shape=out_shape,
        grid_spec=pltpu.PrefetchScalarGridSpec(
            num_scalar_prefetch=1,
            grid=(n_col,),
            in_specs=in_specs,
            out_specs=out_specs,
            scratch_shapes=[pltpu.VMEM((n_col, rows, depth), BF16), pltpu.VMEM((2, rows, wide), F32)],
        ),
        compiler_params=params(1),
        cost_estimate=cost(GATE_UP_COST, 4 * rows * full * wide, 4 * full * wide, 4 * rows * wide),
        name=name,
    )(place, *operands)


def down_call(place, col, pieces, down_weight, n_col, split):
    half, wide = pieces[0].shape
    rows, block = 2 * half, down_weight.shape[1] // n_col
    if split:
        out_shape = [jax.ShapeDtypeStruct((rows, block), BF16)] * n_col
        out_specs = [whole((rows, block))] * n_col
    else:
        out_shape = jax.ShapeDtypeStruct((rows, block * n_col), BF16)
        out_specs = pl.BlockSpec((rows, block), lambda d, place, col: (0, d))
    return pl.pallas_call(
        functools.partial(down_kernel, n_col, split),
        out_shape=out_shape,
        grid_spec=pltpu.PrefetchScalarGridSpec(
            num_scalar_prefetch=2,
            grid=(n_col,),
            in_specs=[whole((half, wide))] * 4 + [pl.BlockSpec(memory_space=pltpu.VMEM)],
            out_specs=out_specs,
            scratch_shapes=[pltpu.VMEM((rows, wide), BF16)] * 2,
        ),
        compiler_params=params(1),
        cost_estimate=cost(DOWN_COST, 4 * rows * wide * block * n_col, 8 * half * wide),
        name="down",
    )(place, col, *pieces, down_weight)


def shifted(x, n, shift):
    return lax.ppermute(x, "col", [(i, (i + shift) % n) for i in range(n)])


def swapped(x, mask):
    return lax.ppermute(x, "row", [(i, i ^ mask) for i in range(4)])


def after(x, *deps):
    return lax.optimization_barrier((x,) + deps)[0]


def pipelined(n_col, tokens, gate_weight, up_weight, down_weight):
    eighth = tokens.shape[0] // 8
    weights = (gate_weight, up_weight)
    down_weight = pltpu.with_memory_space_constraint(down_weight, pltpu.VMEM)
    row, col = lax.axis_index("row"), lax.axis_index("col")
    table = np.array(
        [
            [1 - r % 2, r % 2, r // 2] + [(c - s) % n_col for s in range(n_col)] + list(range(n_col)) + [c]
            for r in range(4)
            for c in range(n_col)
        ],
        np.int32,
    )
    mine = jnp.asarray(table)[row * n_col + col]
    by_shift, col_id = mine[: BLOCKS + n_col], mine[-1:]
    natural = jnp.concatenate([mine[:BLOCKS], mine[BLOCKS + n_col : -1]])

    def direct(piece):
        return [piece] + [shifted(piece, n_col, s) for s in range(1, n_col)]

    bounds = [0, 1, 3, 5, 7, 8]
    def gathered(lo, hi, *behind):
        piece = after(tokens[lo * eighth : hi * eighth], *behind)
        return lax.all_gather(piece, "col", axis=1, tiled=True)

    def gathered(lo, hi, *behind):
        piece = after(tokens[lo * eighth : hi * eighth], *behind)
        return lax.all_gather(piece, "col", axis=1, tiled=True)

    first = direct(tokens[:eighth])
    second = lax.all_gather(tokens[eighth : 3 * eighth], "col", axis=1, tiled=True)
    sources = [(by_shift, first, 0), (natural, [second], 0)]
    chunk_rows = [(b - a) * eighth for a, b in zip(bounds, bounds[1:])]
    last = [mine]

    def partner(i):
        place, tok, block = sources[i]
        out = gate_up_call(after(place, *last), tok, chunk_rows[i], block, weights, n_col, PARTNER, i in SPLIT)
        last[:] = list(out)
        return [swapped(piece, 1) for piece in out]

    def own(i, received):
        place, tok, block = sources[i]
        send, keep = gate_up_call(after(place, *last), tok, chunk_rows[i], block, weights, n_col, OWN, i in SPLIT, received)
        last[:] = [send]
        return keep, swapped(send, 2)

    def gated(pair):
        keep, arrived = after(pair[0], *last), pair[1]
        gate = keep[0].astype(F32) + arrived[0].astype(F32)
        up = keep[1].astype(F32) + arrived[1].astype(F32)
        hidden = (jax.nn.silu(gate) * up).astype(BF16)
        last[:] = [hidden]
        hidden_x = swapped(hidden, 2)
        return hidden, hidden_x, swapped(hidden, 1), swapped(hidden_x, 1)

    def down(pieces, split=False):
        out = down_call(after(by_shift, *last), col_id, pieces, down_weight, n_col, split)
        last[:] = list(out) if split else [out]
        if not split:
            return lax.psum_scatter(out, "col", scatter_dimension=1, tiled=True)
        total = out[-1].astype(F32)
        for s in range(1, n_col):
            total = total + shifted(out[s - 1], n_col, s).astype(F32)
        return total.astype(BF16)

    r0 = partner(0)
    p0 = own(0, r0)
    r1 = partner(1)
    third = gathered(3, 5, second, *last)
    sources.append((natural, [third], 0))
    h0 = gated(p0)
    p1 = own(1, r1)
    r2 = partner(2)
    rest = gathered(5, 8, third, *last)
    sources += [(natural, [rest], 0), (natural, [rest], 2)]
    r3 = partner(3)
    p2 = own(2, r2)
    h1 = gated(p1)
    o0 = down(h0)
    r4 = partner(4)
    p3 = own(3, r3)
    h2 = gated(p2)
    o1 = down(h1)
    p4 = own(4, r4)
    h3 = gated(p3)
    o2 = down(h2)
    h4 = gated(p4)
    o3 = down(h3)
    o4 = down(h4, split=True)
    return jnp.concatenate([o0, o1, o2, o3, o4], axis=0)


def generic(tokens, gate_weight, up_weight, down_weight):
    gathered = lax.all_gather(tokens, "col", axis=1, tiled=True)
    gate = lax.psum_scatter(dot(gathered, gate_weight).astype(BF16), "row", scatter_dimension=0, tiled=True)
    up = lax.psum_scatter(dot(gathered, up_weight).astype(BF16), "row", scatter_dimension=0, tiled=True)
    hidden = (jax.nn.silu(gate.astype(F32)) * up.astype(F32)).astype(BF16)
    hidden = lax.all_gather(hidden, "row", axis=0, tiled=True)
    partial = dot(hidden, down_weight).astype(BF16)
    return lax.psum_scatter(partial, "col", scatter_dimension=1, tiled=True)


def solution(mesh):
    n_row, n_col = mesh.shape["row"], mesh.shape["col"]
    in_specs = (P("groups", ("row", "col")), P("row", "col"), P("row", "col"), P("col", "row"))
    out_specs = P("groups", ("row", "col"))
    step = functools.partial(pipelined, n_col) if n_row == 4 else generic
    return jax.shard_map(step, mesh=mesh, in_specs=in_specs, out_specs=out_specs, check_vma=False)
```

```python
import functools

import jax
import jax.numpy as jnp
import numpy as np
from jax import lax
from jax.experimental import pallas as pl
from jax.experimental.pallas import tpu as pltpu
from jax.sharding import PartitionSpec as P

BF16, F32 = jnp.bfloat16, jnp.float32
GATE_UP_COST, DOWN_COST = 1, 1
SPLIT = (0, 1, 2, 3)
VMEM_LIMIT = 29 * 2**20
PARTNER, OWN, X, BLOCKS = 0, 1, 2, 3


def dot(a, b):
    return jnp.dot(a, b, preferred_element_type=F32)


def accumulate(place, token_refs, gate_ref, up_ref, stage, acc):
    step, depth = pl.program_id(0), gate_ref.shape[0]

    @pl.when(step == 0)
    def _():
        acc[...] = jnp.zeros_like(acc)
        for k in range(stage.shape[0]):
            if len(token_refs) == 1:
                stage[k] = token_refs[0][:, k * depth : (k + 1) * depth]
            else:
                stage[k] = token_refs[k][...]

    tok = stage[step]
    acc[0] += dot(tok, gate_ref[...])
    acc[1] += dot(tok, up_ref[...])


def pieces_of(rows, split):
    half = rows // 2
    if not split:
        return [(slice(0, 2), slice(0, rows))]
    return [(slice(w, w + 1), slice(at, at + half)) for w in (0, 1) for at in (0, half)]


def partner_kernel(n_tok, split, place, *refs):
    token_refs, (gate_ref, up_ref, *out_refs), (stage, acc) = refs[:n_tok], refs[n_tok:-2], refs[-2:]
    accumulate(place, token_refs, gate_ref, up_ref, stage, acc)

    @pl.when(pl.program_id(0) == pl.num_programs(0) - 1)
    def _():
        for (which, rows), out_ref in zip(pieces_of(acc.shape[1], split), out_refs):
            out_ref[...] = acc[which, rows].astype(BF16)


def own_kernel(n_tok, split, place, *refs):
    token_refs, (gate_ref, up_ref, *received_refs) = refs[:n_tok], refs[n_tok:-4]
    send_ref, keep_ref, stage, acc = refs[-4:]
    accumulate(place, token_refs, gate_ref, up_ref, stage, acc)
    half = send_ref.shape[1]

    @pl.when(pl.program_id(0) == pl.num_programs(0) - 1)
    def _():
        for (which, rows), ref in zip(pieces_of(acc.shape[1], split), received_refs):
            acc[which, rows] += ref[...].astype(F32)
        for ref, x in ((send_ref, 1 - place[X]), (keep_ref, place[X])):
            ref[...] = acc[:, pl.ds(pl.multiple_of(x * half, half), half), :].astype(BF16)


def down_kernel(n_col, direct, place, order, own_x, other_x, own_x_core, other_x_core, weight_ref, *rest):
    out_refs, (own_half, partner_half) = rest[:-2], rest[-2:]
    step = pl.program_id(0)
    height, wide = own_x.shape

    @pl.when(step == 0)
    def _():
        for target, mine, other in ((own_half, own_x, other_x), (partner_half, own_x_core, other_x_core)):
            target[pl.ds(pl.multiple_of(place[X] * height, height), height), :] = mine[...]
            target[pl.ds(pl.multiple_of((1 - place[X]) * height, height), height), :] = other[...]

    block = weight_ref.shape[1] // n_col
    columns = pl.ds(pl.multiple_of(order[step] * block, block), block)
    total = dot(own_half[...], weight_ref[pl.ds(pl.multiple_of(place[OWN] * wide, wide), wide), columns])
    total += dot(partner_half[...], weight_ref[pl.ds(pl.multiple_of(place[PARTNER] * wide, wide), wide), columns])
    value = total.astype(BF16)
    each = n_col // len(out_refs)
    for k, out_ref in enumerate(out_refs):
        @pl.when(step // each == k)
        def _(out_ref=out_ref):
            out_ref[...] = value


def whole(shape):
    return pl.BlockSpec(shape, lambda *_: (0,) * len(shape), pipeline_mode=pl.Buffered(1))


def params(n):
    return pltpu.CompilerParams(dimension_semantics=("arbitrary",) * n, vmem_limit_bytes=VMEM_LIMIT)


def cost(scale, flops, *sizes):
    return pl.CostEstimate(flops=int(flops * scale), bytes_accessed=int(sum(sizes) * scale), transcendentals=0)


def gate_up_call(place, tokens, rows, row_block, weights, n_col, which, split, received=None):
    full, wide = weights[0].shape[0], weights[0].shape[1] // 2
    depth, half = full // n_col, rows // 2
    weight = pl.BlockSpec((depth, wide), lambda k, place: (place[BLOCKS + k], place[which]))
    token = pl.BlockSpec(
        (rows, tokens[0].shape[1]), lambda k, place: (row_block, 0), pipeline_mode=pl.Buffered(1)
    )
    in_specs = [token] * len(tokens) + [weight, weight]
    operands = [*tokens, *weights]
    shapes = [(w.stop - w.start, r.stop - r.start, wide) for w, r in pieces_of(rows, split)]
    if received is None:
        body, name = partner_kernel, "partner"
        out_shape, out_specs = [jax.ShapeDtypeStruct(a, BF16) for a in shapes], [whole(a) for a in shapes]
    else:
        body, name = own_kernel, "own"
        out_shape, out_specs = [jax.ShapeDtypeStruct((2, half, wide), BF16)] * 2, [whole((2, half, wide))] * 2
        in_specs += [whole(a) for a in shapes]
        operands += received
    return pl.pallas_call(
        functools.partial(body, len(tokens), split),
        out_shape=out_shape,
        grid_spec=pltpu.PrefetchScalarGridSpec(
            num_scalar_prefetch=1,
            grid=(n_col,),
            in_specs=in_specs,
            out_specs=out_specs,
            scratch_shapes=[pltpu.VMEM((n_col, rows, depth), BF16), pltpu.VMEM((2, rows, wide), F32)],
        ),
        compiler_params=params(1),
        cost_estimate=cost(GATE_UP_COST, 4 * rows * full * wide, 4 * full * wide, 4 * rows * wide),
        name=name,
    )(place, *operands)


def down_call(place, order, pieces, down_weight, n_col, direct):
    half, wide = pieces[0].shape
    rows, block = 2 * half, down_weight.shape[1] // n_col
    if direct:
        out_shape = [jax.ShapeDtypeStruct((rows, block), BF16)] * n_col
        out_specs = [whole((rows, block))] * n_col
    else:
        out_shape = [jax.ShapeDtypeStruct((rows, 2 * block), BF16)] * 2
        out_specs = [
            pl.BlockSpec((rows, block), lambda d, place, order: (0, jnp.minimum(d, 1))),
            pl.BlockSpec((rows, block), lambda d, place, order: (0, jnp.maximum(d - 2, 0))),
        ]
    return pl.pallas_call(
        functools.partial(down_kernel, n_col, direct),
        out_shape=out_shape,
        grid_spec=pltpu.PrefetchScalarGridSpec(
            num_scalar_prefetch=2,
            grid=(n_col,),
            in_specs=[whole((half, wide))] * 4 + [pl.BlockSpec(memory_space=pltpu.VMEM)],
            out_specs=out_specs,
            scratch_shapes=[pltpu.VMEM((rows, wide), BF16)] * 2,
        ),
        compiler_params=params(1),
        cost_estimate=cost(DOWN_COST, 4 * rows * wide * block * n_col, 8 * half * wide),
        name="down",
    )(place, order, *pieces, down_weight)


def shifted(x, n, shift):
    return lax.ppermute(x, "col", [(i, (i + shift) % n) for i in range(n)])


def swapped(x, mask):
    return lax.ppermute(x, "row", [(i, i ^ mask) for i in range(4)])


def after(x, *deps):
    return lax.optimization_barrier((x,) + deps)[0]


def pipelined(tokens, gate_weight, up_weight, down_weight):
    n_col = 4
    eighth = tokens.shape[0] // 8
    weights = (gate_weight, up_weight)
    down_weight = pltpu.with_memory_space_constraint(down_weight, pltpu.VMEM)
    table = np.array(
        [
            [[1 - r % 2, r % 2, r // 2] + [(c - s) % n_col for s in range(n_col)] + [0]]
            + [[c ^ 1, c ^ 3, c, c ^ 2] * 2, [(c + 1) % n_col, (c + 2) % n_col, (c + 3) % n_col, c] * 2]
            for r in range(4)
            for c in range(n_col)
        ],
        np.int32,
    )
    mine = jnp.asarray(table)[lax.axis_index("row") * n_col + lax.axis_index("col")]
    place, halving, straight = mine[0], mine[1], mine[2]
    last = [place]

    def send_tokens(lo, hi):
        piece = after(tokens[lo * eighth : hi * eighth], *last)
        return [piece] + [shifted(piece, n_col, s) for s in range(1, n_col)]

    def partner(i):
        tok, rows, block = sources[i]
        out = gate_up_call(after(place, *last), tok, rows, block, weights, n_col, PARTNER, i in SPLIT)
        last[:] = list(out)
        return [swapped(piece, 1) for piece in out]

    def own(i, received):
        tok, rows, block = sources[i]
        send, keep = gate_up_call(after(place, *last), tok, rows, block, weights, n_col, OWN, i in SPLIT, received)
        last[:] = [send]
        return keep, swapped(send, 2)

    def gated(pair):
        keep, arrived = after(pair[0], *last), pair[1]
        gate = keep[0].astype(F32) + arrived[0].astype(F32)
        up = keep[1].astype(F32) + arrived[1].astype(F32)
        hidden = (jax.nn.silu(gate) * up).astype(BF16)
        last[:] = [hidden]
        return hidden, swapped(hidden, 2), swapped(hidden, 1)

    def relay(pieces):
        hidden, hidden_x, hidden_core = pieces
        return hidden, hidden_x, hidden_core, swapped(after(hidden_x, *last), 1)

    def down(pieces):
        send, keep = down_call(after(place, *last), halving, pieces, down_weight, n_col, False)
        last[:] = [send]
        return keep, lax.ppermute(send, "col", [(c, c ^ 1) for c in range(n_col)])

    def halve(pair):
        keep, arrived = after(pair[0], *last), pair[1]
        block = keep.shape[1] // 2
        total = [keep[:, at : at + block].astype(F32) + arrived[:, at : at + block].astype(F32) for at in (0, block)]
        send = total[1].astype(BF16)
        last[:] = [send]
        return total[0], lax.ppermute(send, "col", [(c, c ^ 2) for c in range(n_col)])

    def down_direct(pieces):
        out = down_call(after(place, *last), straight, pieces, down_weight, n_col, True)
        total = out[-1].astype(F32)
        for s in range(1, n_col):
            total = total + shifted(out[s - 1], n_col, s).astype(F32)
        return total.astype(BF16)

    def finish(pair):
        return (pair[0] + pair[1].astype(F32)).astype(BF16)

    t0, t1 = send_tokens(0, 1), send_tokens(1, 3)
    sources = [(t0, eighth, 0), (t1, 2 * eighth, 0)]
    r0 = partner(0)
    t2 = send_tokens(3, 5)
    p0 = own(0, r0)
    r1 = partner(1)
    h0 = gated(p0)
    p1 = own(1, r1)
    t3 = send_tokens(5, 8)
    sources += [(t2, 2 * eighth, 0), (t3, 2 * eighth, 0), (t3, eighth, 2)]
    r2 = partner(2)
    h0 = relay(h0)
    d0 = down(h0)
    p2 = own(2, r2)
    h1 = gated(p1)
    r3 = partner(3)
    z0 = halve(d0)
    p3 = own(3, r3)
    h1 = relay(h1)
    h2 = gated(p2)
    r4 = partner(4)
    d1 = down(h1)
    p4 = own(4, r4)
    z1 = halve(d1)
    h2 = relay(h2)
    h3 = gated(p3)
    d2 = down(h2)
    h3 = relay(h3)
    h4 = gated(p4)
    z2 = halve(d2)
    d3 = down(h3)
    h4 = relay(h4)
    z3 = halve(d3)
    o4 = down_direct(h4)
    return jnp.concatenate([finish(z0), finish(z1), finish(z2), finish(z3), o4], axis=0)


def generic(tokens, gate_weight, up_weight, down_weight):
    gathered = lax.all_gather(tokens, "col", axis=1, tiled=True)
    gate = lax.psum_scatter(dot(gathered, gate_weight).astype(BF16), "row", scatter_dimension=0, tiled=True)
    up = lax.psum_scatter(dot(gathered, up_weight).astype(BF16), "row", scatter_dimension=0, tiled=True)
    hidden = (jax.nn.silu(gate.astype(F32)) * up.astype(F32)).astype(BF16)
    hidden = lax.all_gather(hidden, "row", axis=0, tiled=True)
    partial = dot(hidden, down_weight).astype(BF16)
    return lax.psum_scatter(partial, "col", scatter_dimension=1, tiled=True)


def solution(mesh):
    n_row, n_col = mesh.shape["row"], mesh.shape["col"]
    in_specs = (P("groups", ("row", "col")), P("row", "col"), P("row", "col"), P("col", "row"))
    out_specs = P("groups", ("row", "col"))
    step = pipelined if (n_row, n_col) == (4, 4) else generic
    return jax.shard_map(step, mesh=mesh, in_specs=in_specs, out_specs=out_specs, check_vma=False)
```

```python
import functools

import jax
import jax.numpy as jnp
import numpy as np
from jax import lax
from jax.experimental import pallas as pl
from jax.experimental.pallas import tpu as pltpu
from jax.sharding import PartitionSpec as P

BF16, F32 = jnp.bfloat16, jnp.float32
FIRST_COST, GATE_UP_COST, DOWN_COST = 0.2, 0.2, 0.2
SPLIT = (4, 4, 4, 2, 2)
VMEM_LIMIT = 29 * 2**20
PARTNER, OWN, X, BLOCKS = 0, 1, 2, 3


def dot(a, b):
    return jnp.dot(a, b, preferred_element_type=F32)


def accumulate(place, token_refs, gate_ref, up_ref, stage, acc):
    step, depth = pl.program_id(0), gate_ref.shape[0]

    @pl.when(step == 0)
    def _():
        acc[...] = jnp.zeros_like(acc)
        for k in range(stage.shape[0]):
            if len(token_refs) == 1:
                stage[k] = token_refs[0][:, k * depth : (k + 1) * depth]
            else:
                stage[k] = token_refs[k][...]

    tok = stage[step]
    acc[0] += dot(tok, gate_ref[...])
    acc[1] += dot(tok, up_ref[...])


def pieces_of(rows, split):
    if split == 1:
        return [(slice(0, 2), slice(0, rows))]
    height = 2 * rows // split
    return [(slice(w, w + 1), slice(at, at + height)) for w in (0, 1) for at in range(0, rows, height)]


def partner_kernel(n_tok, split, place, *refs):
    token_refs, (gate_ref, up_ref, *out_refs), (stage, acc) = refs[:n_tok], refs[n_tok:-2], refs[-2:]
    accumulate(place, token_refs, gate_ref, up_ref, stage, acc)

    @pl.when(pl.program_id(0) == pl.num_programs(0) - 1)
    def _():
        for (which, rows), out_ref in zip(pieces_of(acc.shape[1], split), out_refs):
            out_ref[...] = acc[which, rows].astype(BF16)


def own_kernel(n_tok, split, place, *refs):
    token_refs, (gate_ref, up_ref, *received_refs) = refs[:n_tok], refs[n_tok:-4]
    send_ref, keep_ref, stage, acc = refs[-4:]
    accumulate(place, token_refs, gate_ref, up_ref, stage, acc)
    half = send_ref.shape[1]

    @pl.when(pl.program_id(0) == pl.num_programs(0) - 1)
    def _():
        for (which, rows), ref in zip(pieces_of(acc.shape[1], split), received_refs):
            acc[which, rows] += ref[...].astype(F32)
        for ref, x in ((send_ref, 1 - place[X]), (keep_ref, place[X])):
            ref[...] = acc[:, pl.ds(pl.multiple_of(x * half, half), half), :].astype(BF16)


def down_kernel(n_col, direct, place, order, own_x, other_x, own_x_core, other_x_core, weight_ref, *rest):
    out_refs, (own_half, partner_half) = rest[:-2], rest[-2:]
    step = pl.program_id(0)
    height, wide = own_x.shape

    @pl.when(step == 0)
    def _():
        for target, mine, other in ((own_half, own_x, other_x), (partner_half, own_x_core, other_x_core)):
            target[pl.ds(pl.multiple_of(place[X] * height, height), height), :] = mine[...]
            target[pl.ds(pl.multiple_of((1 - place[X]) * height, height), height), :] = other[...]

    block = weight_ref.shape[1] // n_col
    columns = pl.ds(pl.multiple_of(order[step] * block, block), block)
    total = dot(own_half[...], weight_ref[pl.ds(pl.multiple_of(place[OWN] * wide, wide), wide), columns])
    total += dot(partner_half[...], weight_ref[pl.ds(pl.multiple_of(place[PARTNER] * wide, wide), wide), columns])
    value = total.astype(BF16)
    each = n_col // len(out_refs)
    for k, out_ref in enumerate(out_refs):
        @pl.when(step // each == k)
        def _(out_ref=out_ref):
            out_ref[...] = value


def whole(shape):
    return pl.BlockSpec(shape, lambda *_: (0,) * len(shape), pipeline_mode=pl.Buffered(1))


def params(n):
    return pltpu.CompilerParams(dimension_semantics=("arbitrary",) * n, vmem_limit_bytes=VMEM_LIMIT)


def cost(scale, flops, *sizes):
    return pl.CostEstimate(flops=int(flops * scale), bytes_accessed=int(sum(sizes) * scale), transcendentals=0)


def gate_up_call(place, tokens, rows, row_block, weights, n_col, which, split, scale, received=None):
    full, wide = weights[0].shape[0], weights[0].shape[1] // 2
    depth, half = full // n_col, rows // 2
    weight = pl.BlockSpec((depth, wide), lambda k, place: (place[BLOCKS + k], place[which]))
    token = pl.BlockSpec(
        (rows, tokens[0].shape[1]), lambda k, place: (row_block, 0), pipeline_mode=pl.Buffered(1)
    )
    in_specs = [token] * len(tokens) + [weight, weight]
    operands = [*tokens, *weights]
    shapes = [(w.stop - w.start, r.stop - r.start, wide) for w, r in pieces_of(rows, split)]
    if received is None:
        body, name = partner_kernel, "partner"
        out_shape, out_specs = [jax.ShapeDtypeStruct(a, BF16) for a in shapes], [whole(a) for a in shapes]
    else:
        body, name = own_kernel, "own"
        out_shape, out_specs = [jax.ShapeDtypeStruct((2, half, wide), BF16)] * 2, [whole((2, half, wide))] * 2
        in_specs += [whole(a) for a in shapes]
        operands += received
    return pl.pallas_call(
        functools.partial(body, len(tokens), split),
        out_shape=out_shape,
        grid_spec=pltpu.PrefetchScalarGridSpec(
            num_scalar_prefetch=1,
            grid=(n_col,),
            in_specs=in_specs,
            out_specs=out_specs,
            scratch_shapes=[pltpu.VMEM((n_col, rows, depth), BF16), pltpu.VMEM((2, rows, wide), F32)],
        ),
        compiler_params=params(1),
        cost_estimate=cost(scale, 4 * rows * full * wide, 4 * full * wide, 4 * rows * wide),
        name=name,
    )(place, *operands)


def down_call(place, order, pieces, down_weight, n_col, direct):
    half, wide = pieces[0].shape
    rows, block = 2 * half, down_weight.shape[1] // n_col
    if direct:
        out_shape = [jax.ShapeDtypeStruct((rows, block), BF16)] * n_col
        out_specs = [whole((rows, block))] * n_col
    else:
        out_shape = [jax.ShapeDtypeStruct((rows, 2 * block), BF16)] * 2
        out_specs = [
            pl.BlockSpec((rows, block), lambda d, place, order: (0, jnp.minimum(d, 1))),
            pl.BlockSpec((rows, block), lambda d, place, order: (0, jnp.maximum(d - 2, 0))),
        ]
    return pl.pallas_call(
        functools.partial(down_kernel, n_col, direct),
        out_shape=out_shape,
        grid_spec=pltpu.PrefetchScalarGridSpec(
            num_scalar_prefetch=2,
            grid=(n_col,),
            in_specs=[whole((half, wide))] * 4 + [pl.BlockSpec(memory_space=pltpu.VMEM)],
            out_specs=out_specs,
            scratch_shapes=[pltpu.VMEM((rows, wide), BF16)] * 2,
        ),
        compiler_params=params(1),
        cost_estimate=cost(DOWN_COST, 4 * rows * wide * block * n_col, 8 * half * wide),
        name="down",
    )(place, order, *pieces, down_weight)


def shifted(x, n, shift):
    return lax.ppermute(x, "col", [(i, (i + shift) % n) for i in range(n)])


def swapped(x, mask):
    return lax.ppermute(x, "row", [(i, i ^ mask) for i in range(4)])


def after(x, *deps):
    return lax.optimization_barrier((x,) + deps)[0]


def pipelined(tokens, gate_weight, up_weight, down_weight):
    n_col = 4
    eighth = tokens.shape[0] // 8
    weights = (gate_weight, up_weight)
    down_weight = pltpu.with_memory_space_constraint(down_weight, pltpu.VMEM)
    table = np.array(
        [
            [[1 - r % 2, r % 2, r // 2] + [(c - s) % n_col for s in range(n_col)] + [0]]
            + [[1 - r % 2, r % 2, r // 2] + list(range(n_col)) + [0]]
            + [[c ^ 1, c ^ 3, c, c ^ 2] * 2, [(c + 1) % n_col, (c + 2) % n_col, (c + 3) % n_col, c] * 2]
            for r in range(4)
            for c in range(n_col)
        ],
        np.int32,
    )
    mine = jnp.asarray(table)[lax.axis_index("row") * n_col + lax.axis_index("col")]
    by_shift, natural, halving, straight = (mine[k] for k in range(4))
    place = natural
    last = [place]

    def scale(i):
        return FIRST_COST if i == 0 else GATE_UP_COST

    def partner(i):
        where, tok, rows, block = sources[i]
        out = gate_up_call(after(where, *last), tok, rows, block, weights, n_col, PARTNER, SPLIT[i], scale(i))
        last[:] = list(out)
        return [swapped(piece, 1) for piece in out]

    def own(i, received):
        where, tok, rows, block = sources[i]
        send, keep = gate_up_call(after(where, *last), tok, rows, block, weights, n_col, OWN, SPLIT[i], scale(i), received)
        last[:] = [send]
        return keep, swapped(send, 2)

    def gated(pair):
        keep, arrived = after(pair[0], *last), pair[1]
        gate = keep[0].astype(F32) + arrived[0].astype(F32)
        up = keep[1].astype(F32) + arrived[1].astype(F32)
        hidden = (jax.nn.silu(gate) * up).astype(BF16)
        last[:] = [hidden]
        return hidden, swapped(hidden, 2), swapped(hidden, 1)

    def relay(pieces):
        hidden, hidden_x, hidden_core = pieces
        return hidden, hidden_x, hidden_core, swapped(after(hidden_x, *last), 1)

    def down(pieces):
        send, keep = down_call(after(place, *last), halving, pieces, down_weight, n_col, False)
        last[:] = [send]
        return keep, lax.ppermute(send, "col", [(c, c ^ 1) for c in range(n_col)])

    def halve(pair):
        keep, arrived = after(pair[0], *last), pair[1]
        block = keep.shape[1] // 2
        total = [keep[:, at : at + block].astype(F32) + arrived[:, at : at + block].astype(F32) for at in (0, block)]
        send = total[1].astype(BF16)
        last[:] = [send]
        return total[0], lax.ppermute(send, "col", [(c, c ^ 2) for c in range(n_col)])

    def down_direct(pieces):
        out = down_call(after(place, *last), straight, pieces, down_weight, n_col, True)
        last[:] = out
        total = out[-1].astype(F32)
        for s in range(1, n_col):
            total = total + shifted(out[s - 1], n_col, s).astype(F32)
        return total.astype(BF16)

    def finish(pair):
        out = (after(pair[0], *last) + pair[1].astype(F32)).astype(BF16)
        last[:] = [out]
        return out

    first = [tokens[: 2 * eighth]]
    first += [shifted(first[0], n_col, s) for s in range(1, n_col)]
    rest = [lax.all_gather(tokens[2 * eighth :], "col", axis=1, tiled=True)]
    sources = [
        (by_shift, first, 2 * eighth, 0),
        (natural, rest, 2 * eighth, 0),
        (natural, rest, 2 * eighth, 1),
        (natural, rest, eighth, 4),
        (natural, rest, eighth, 5),
    ]
    r0 = partner(0)
    p0 = own(0, r0)
    r1 = partner(1)
    h0 = gated(p0)
    p1 = own(1, r1)
    h0 = relay(h0)
    d0 = down(h0)
    r2 = partner(2)
    z0 = halve(d0)
    h1 = gated(p1)
    p2 = own(2, r2)
    h1 = relay(h1)
    d1 = down(h1)
    r3 = partner(3)
    o0 = finish(z0)
    r4 = partner(4)
    z1 = halve(d1)
    h2 = gated(p2)
    p3 = own(3, r3)
    p4 = own(4, r4)
    o1 = finish(z1)
    h2 = relay(h2)
    d2 = down(h2)
    h3 = gated(p3)
    h4 = gated(p4)
    h3 = relay(h3)
    z2 = halve(d2)
    d3 = down(h3)
    h4 = relay(h4)
    o4 = down_direct(h4)
    o2 = finish(z2)
    z3 = halve(d3)
    return jnp.concatenate([o0, o1, o2, finish(z3), o4], axis=0)


def generic(tokens, gate_weight, up_weight, down_weight):
    gathered = lax.all_gather(tokens, "col", axis=1, tiled=True)
    gate = lax.psum_scatter(dot(gathered, gate_weight).astype(BF16), "row", scatter_dimension=0, tiled=True)
    up = lax.psum_scatter(dot(gathered, up_weight).astype(BF16), "row", scatter_dimension=0, tiled=True)
    hidden = (jax.nn.silu(gate.astype(F32)) * up.astype(F32)).astype(BF16)
    hidden = lax.all_gather(hidden, "row", axis=0, tiled=True)
    partial = dot(hidden, down_weight).astype(BF16)
    return lax.psum_scatter(partial, "col", scatter_dimension=1, tiled=True)


def solution(mesh):
    n_row, n_col = mesh.shape["row"], mesh.shape["col"]
    in_specs = (P("groups", ("row", "col")), P("row", "col"), P("row", "col"), P("col", "row"))
    out_specs = P("groups", ("row", "col"))
    step = pipelined if (n_row, n_col) == (4, 4) else generic
    return jax.shard_map(step, mesh=mesh, in_specs=in_specs, out_specs=out_specs, check_vma=False)
```

```python
import functools

import jax
import jax.numpy as jnp
import numpy as np
from jax import lax
from jax.experimental import pallas as pl
from jax.experimental.pallas import tpu as pltpu
from jax.sharding import PartitionSpec as P

BF16, F32 = jnp.bfloat16, jnp.float32
FIRST_COST, GATE_UP_COST, DOWN_COST = 1, 0.2, 0.2
SPLIT = (4, 4, 4, 4, 1)
VMEM_LIMIT = 29 * 2**20
PARTNER, OWN, X, BLOCKS = 0, 1, 2, 3


def dot(a, b):
    return jnp.dot(a, b, preferred_element_type=F32)


def accumulate(place, token_refs, gate_ref, up_ref, stage, acc):
    step, depth = pl.program_id(0), gate_ref.shape[0]

    @pl.when(step == 0)
    def _():
        acc[...] = jnp.zeros_like(acc)
        for k in range(stage.shape[0]):
            if len(token_refs) == 1:
                stage[k] = token_refs[0][:, k * depth : (k + 1) * depth]
            else:
                stage[k] = token_refs[k][...]

    tok = stage[step]
    acc[0] += dot(tok, gate_ref[...])
    acc[1] += dot(tok, up_ref[...])


def pieces_of(rows, split):
    if split == 1:
        return [(slice(0, 2), slice(0, rows))]
    height = 2 * rows // split
    return [(slice(w, w + 1), slice(at, at + height)) for w in (0, 1) for at in range(0, rows, height)]


def partner_kernel(n_tok, split, place, *refs):
    token_refs, (gate_ref, up_ref, *out_refs), (stage, acc) = refs[:n_tok], refs[n_tok:-2], refs[-2:]
    accumulate(place, token_refs, gate_ref, up_ref, stage, acc)

    @pl.when(pl.program_id(0) == pl.num_programs(0) - 1)
    def _():
        for (which, rows), out_ref in zip(pieces_of(acc.shape[1], split), out_refs):
            out_ref[...] = acc[which, rows].astype(BF16)


def own_kernel(n_tok, split, place, *refs):
    token_refs, (gate_ref, up_ref, *received_refs) = refs[:n_tok], refs[n_tok:-4]
    send_ref, keep_ref, stage, acc = refs[-4:]
    accumulate(place, token_refs, gate_ref, up_ref, stage, acc)
    half = send_ref.shape[1]

    @pl.when(pl.program_id(0) == pl.num_programs(0) - 1)
    def _():
        for (which, rows), ref in zip(pieces_of(acc.shape[1], split), received_refs):
            acc[which, rows] += ref[...].astype(F32)
        for ref, x in ((send_ref, 1 - place[X]), (keep_ref, place[X])):
            ref[...] = acc[:, pl.ds(pl.multiple_of(x * half, half), half), :].astype(BF16)


def down_kernel(n_col, direct, place, order, own_x, other_x, own_x_core, other_x_core, weight_ref, *rest):
    out_refs, (own_half, partner_half) = rest[:-2], rest[-2:]
    step = pl.program_id(0)
    height, wide = own_x.shape

    @pl.when(step == 0)
    def _():
        for target, mine, other in ((own_half, own_x, other_x), (partner_half, own_x_core, other_x_core)):
            target[pl.ds(pl.multiple_of(place[X] * height, height), height), :] = mine[...]
            target[pl.ds(pl.multiple_of((1 - place[X]) * height, height), height), :] = other[...]

    block = weight_ref.shape[1] // n_col
    columns = pl.ds(pl.multiple_of(order[step] * block, block), block)
    total = dot(own_half[...], weight_ref[pl.ds(pl.multiple_of(place[OWN] * wide, wide), wide), columns])
    total += dot(partner_half[...], weight_ref[pl.ds(pl.multiple_of(place[PARTNER] * wide, wide), wide), columns])
    value = total.astype(BF16)
    each = n_col // len(out_refs)
    for k, out_ref in enumerate(out_refs):
        @pl.when(step // each == k)
        def _(out_ref=out_ref):
            out_ref[...] = value


def whole(shape):
    return pl.BlockSpec(shape, lambda *_: (0,) * len(shape), pipeline_mode=pl.Buffered(1))


def params(n):
    return pltpu.CompilerParams(dimension_semantics=("arbitrary",) * n, vmem_limit_bytes=VMEM_LIMIT)


def cost(scale, flops, *sizes):
    return pl.CostEstimate(flops=int(flops * scale), bytes_accessed=int(sum(sizes) * scale), transcendentals=0)


def gate_up_call(place, tokens, rows, row_block, weights, n_col, which, split, scale, received=None):
    full, wide = weights[0].shape[0], weights[0].shape[1] // 2
    depth, half = full // n_col, rows // 2
    weight = pl.BlockSpec((depth, wide), lambda k, place: (place[BLOCKS + k], place[which]))
    token = pl.BlockSpec(
        (rows, tokens[0].shape[1]), lambda k, place: (row_block, 0), pipeline_mode=pl.Buffered(1)
    )
    in_specs = [token] * len(tokens) + [weight, weight]
    operands = [*tokens, *weights]
    shapes = [(w.stop - w.start, r.stop - r.start, wide) for w, r in pieces_of(rows, split)]
    if received is None:
        body, name = partner_kernel, "partner"
        out_shape, out_specs = [jax.ShapeDtypeStruct(a, BF16) for a in shapes], [whole(a) for a in shapes]
    else:
        body, name = own_kernel, "own"
        out_shape, out_specs = [jax.ShapeDtypeStruct((2, half, wide), BF16)] * 2, [whole((2, half, wide))] * 2
        in_specs += [whole(a) for a in shapes]
        operands += received
    return pl.pallas_call(
        functools.partial(body, len(tokens), split),
        out_shape=out_shape,
        grid_spec=pltpu.PrefetchScalarGridSpec(
            num_scalar_prefetch=1,
            grid=(n_col,),
            in_specs=in_specs,
            out_specs=out_specs,
            scratch_shapes=[pltpu.VMEM((n_col, rows, depth), BF16), pltpu.VMEM((2, rows, wide), F32)],
        ),
        compiler_params=params(1),
        cost_estimate=cost(scale, 4 * rows * full * wide, 4 * full * wide, 4 * rows * wide),
        name=name,
    )(place, *operands)


def down_call(place, order, pieces, down_weight, n_col, direct):
    half, wide = pieces[0].shape
    rows, block = 2 * half, down_weight.shape[1] // n_col
    if direct:
        out_shape = [jax.ShapeDtypeStruct((rows, block), BF16)] * n_col
        out_specs = [whole((rows, block))] * n_col
    else:
        out_shape = [jax.ShapeDtypeStruct((rows, 2 * block), BF16)] * 2
        out_specs = [
            pl.BlockSpec((rows, block), lambda d, place, order: (0, jnp.minimum(d, 1))),
            pl.BlockSpec((rows, block), lambda d, place, order: (0, jnp.maximum(d - 2, 0))),
        ]
    return pl.pallas_call(
        functools.partial(down_kernel, n_col, direct),
        out_shape=out_shape,
        grid_spec=pltpu.PrefetchScalarGridSpec(
            num_scalar_prefetch=2,
            grid=(n_col,),
            in_specs=[whole((half, wide))] * 4 + [pl.BlockSpec(memory_space=pltpu.VMEM)],
            out_specs=out_specs,
            scratch_shapes=[pltpu.VMEM((rows, wide), BF16)] * 2,
        ),
        compiler_params=params(1),
        cost_estimate=cost(DOWN_COST, 4 * rows * wide * block * n_col, 8 * half * wide),
        name="down",
    )(place, order, *pieces, down_weight)


def shifted(x, n, shift):
    return lax.ppermute(x, "col", [(i, (i + shift) % n) for i in range(n)])


def swapped(x, mask):
    return lax.ppermute(x, "row", [(i, i ^ mask) for i in range(4)])


def after(x, *deps):
    return lax.optimization_barrier((x,) + deps)[0]


def pipelined(tokens, gate_weight, up_weight, down_weight):
    n_col = 4
    eighth = tokens.shape[0] // 8
    weights = (gate_weight, up_weight)
    down_weight = pltpu.with_memory_space_constraint(down_weight, pltpu.VMEM)
    table = np.array(
        [
            [[1 - r % 2, r % 2, r // 2] + [(c - s) % n_col for s in range(n_col)] + [0]]
            + [[c ^ 1, c ^ 3, c, c ^ 2] * 2, [(c + 1) % n_col, (c + 2) % n_col, (c + 3) % n_col, c] * 2]
            for r in range(4)
            for c in range(n_col)
        ],
        np.int32,
    )
    mine = jnp.asarray(table)[lax.axis_index("row") * n_col + lax.axis_index("col")]
    place, halving, straight = mine[0], mine[1], mine[2]
    last = [place]

    def send_tokens(lo, hi):
        piece = after(tokens[lo * eighth : hi * eighth], *last)
        return [piece] + [shifted(piece, n_col, s) for s in range(1, n_col)]

    def scale(i, which):
        return FIRST_COST if i == 0 or (i, which) == (1, PARTNER) else GATE_UP_COST

    def partner(i):
        tok, rows, block = sources[i]
        out = gate_up_call(after(place, *last), tok, rows, block, weights, n_col, PARTNER, SPLIT[i], scale(i, PARTNER))
        last[:] = list(out)
        return [swapped(piece, 1) for piece in out]

    def own(i, received):
        tok, rows, block = sources[i]
        send, keep = gate_up_call(after(place, *last), tok, rows, block, weights, n_col, OWN, SPLIT[i], scale(i, OWN), received)
        last[:] = [send]
        return keep, swapped(send, 2)

    def gated(pair):
        keep, arrived = after(pair[0], *last), pair[1]
        gate = keep[0].astype(F32) + arrived[0].astype(F32)
        up = keep[1].astype(F32) + arrived[1].astype(F32)
        hidden = (jax.nn.silu(gate) * up).astype(BF16)
        last[:] = [hidden]
        return hidden, swapped(hidden, 2), swapped(hidden, 1)

    def relay(pieces):
        hidden, hidden_x, hidden_core = pieces
        return hidden, hidden_x, hidden_core, swapped(after(hidden_x, *last), 1)

    def down(pieces):
        send, keep = down_call(after(place, *last), halving, pieces, down_weight, n_col, False)
        last[:] = [send]
        return keep, lax.ppermute(send, "col", [(c, c ^ 1) for c in range(n_col)])

    def halve(pair):
        keep, arrived = after(pair[0], *last), pair[1]
        block = keep.shape[1] // 2
        total = [keep[:, at : at + block].astype(F32) + arrived[:, at : at + block].astype(F32) for at in (0, block)]
        send = total[1].astype(BF16)
        last[:] = [send]
        return total[0], lax.ppermute(send, "col", [(c, c ^ 2) for c in range(n_col)])

    def down_direct(pieces):
        out = down_call(after(place, *last), straight, pieces, down_weight, n_col, True)
        last[:] = out
        total = out[-1].astype(F32)
        for s in range(1, n_col):
            total = total + shifted(out[s - 1], n_col, s).astype(F32)
        return total.astype(BF16)

    def finish(pair):
        out = (after(pair[0], *last) + pair[1].astype(F32)).astype(BF16)
        last[:] = [out]
        return out

    t0, t1 = send_tokens(0, 1), send_tokens(1, 3)
    sources = [(t0, eighth, 0), (t1, 2 * eighth, 0)]
    r0 = partner(0)
    t2 = send_tokens(3, 5)
    p0 = own(0, r0)
    r1 = partner(1)
    h0 = gated(p0)
    p1 = own(1, r1)
    t3 = send_tokens(5, 8)
    sources += [(t2, 2 * eighth, 0), (t3, 2 * eighth, 0), (t3, eighth, 2)]
    r2 = partner(2)
    h0 = relay(h0)
    d0 = down(h0)
    p2 = own(2, r2)
    h1 = gated(p1)
    r3 = partner(3)
    z0 = halve(d0)
    p3 = own(3, r3)
    h1 = relay(h1)
    h2 = gated(p2)
    r4 = partner(4)
    o0 = finish(z0)
    d1 = down(h1)
    p4 = own(4, r4)
    z1 = halve(d1)
    h2 = relay(h2)
    h3 = gated(p3)
    d2 = down(h2)
    o1 = finish(z1)
    h3 = relay(h3)
    h4 = gated(p4)
    z2 = halve(d2)
    d3 = down(h3)
    h4 = relay(h4)
    o4 = down_direct(h4)
    o2 = finish(z2)
    z3 = halve(d3)
    return jnp.concatenate([o0, o1, o2, finish(z3), o4], axis=0)


def generic(tokens, gate_weight, up_weight, down_weight):
    gathered = lax.all_gather(tokens, "col", axis=1, tiled=True)
    gate = lax.psum_scatter(dot(gathered, gate_weight).astype(BF16), "row", scatter_dimension=0, tiled=True)
    up = lax.psum_scatter(dot(gathered, up_weight).astype(BF16), "row", scatter_dimension=0, tiled=True)
    hidden = (jax.nn.silu(gate.astype(F32)) * up.astype(F32)).astype(BF16)
    hidden = lax.all_gather(hidden, "row", axis=0, tiled=True)
    partial = dot(hidden, down_weight).astype(BF16)
    return lax.psum_scatter(partial, "col", scatter_dimension=1, tiled=True)


def solution(mesh):
    n_row, n_col = mesh.shape["row"], mesh.shape["col"]
    in_specs = (P("groups", ("row", "col")), P("row", "col"), P("row", "col"), P("col", "row"))
    out_specs = P("groups", ("row", "col"))
    step = pipelined if (n_row, n_col) == (4, 4) else generic
    return jax.shard_map(step, mesh=mesh, in_specs=in_specs, out_specs=out_specs, check_vma=False)
```

```python
import functools

import jax
import jax.numpy as jnp
import numpy as np
from jax import lax
from jax.experimental import pallas as pl
from jax.experimental.pallas import tpu as pltpu
from jax.sharding import PartitionSpec as P

BF16, F32 = jnp.bfloat16, jnp.float32
FIRST_COST, GATE_UP_COST, DOWN_COST = 1, 0.2, 0.2
SPLIT = (4, 4, 4, 4, 1)
MIB, GATE_UP_VMEM, DOWN_VMEM = 2**20, 29, 29
PARTNER, OWN, X, BLOCKS = 0, 1, 2, 3


def dot(a, b):
    return jnp.dot(a, b, preferred_element_type=F32)


def accumulate(place, token_refs, gate_ref, up_ref, stage, acc):
    step, depth = pl.program_id(0), gate_ref.shape[0]

    @pl.when(step == 0)
    def _():
        acc[...] = jnp.zeros_like(acc)
        for k in range(stage.shape[0]):
            if len(token_refs) == 1:
                stage[k] = token_refs[0][:, k * depth : (k + 1) * depth]
            else:
                stage[k] = token_refs[k][...]

    tok = stage[step]
    acc[0] += dot(tok, gate_ref[...])
    acc[1] += dot(tok, up_ref[...])


def pieces_of(rows, split):
    if split == 1:
        return [(slice(0, 2), slice(0, rows))]
    height = 2 * rows // split
    return [(slice(w, w + 1), slice(at, at + height)) for w in (0, 1) for at in range(0, rows, height)]


def partner_kernel(n_tok, split, place, *refs):
    token_refs, (gate_ref, up_ref, *out_refs), (stage, acc) = refs[:n_tok], refs[n_tok:-2], refs[-2:]
    accumulate(place, token_refs, gate_ref, up_ref, stage, acc)

    @pl.when(pl.program_id(0) == pl.num_programs(0) - 1)
    def _():
        for (which, rows), out_ref in zip(pieces_of(acc.shape[1], split), out_refs):
            out_ref[...] = acc[which, rows].astype(BF16)


def own_kernel(n_tok, split, place, *refs):
    token_refs, (gate_ref, up_ref, *received_refs) = refs[:n_tok], refs[n_tok:-4]
    send_ref, keep_ref, stage, acc = refs[-4:]
    accumulate(place, token_refs, gate_ref, up_ref, stage, acc)
    half = send_ref.shape[1]

    @pl.when(pl.program_id(0) == pl.num_programs(0) - 1)
    def _():
        for (which, rows), ref in zip(pieces_of(acc.shape[1], split), received_refs):
            acc[which, rows] += ref[...].astype(F32)
        for ref, x in ((send_ref, 1 - place[X]), (keep_ref, place[X])):
            ref[...] = acc[:, pl.ds(pl.multiple_of(x * half, half), half), :].astype(BF16)


def down_kernel(n_col, direct, place, order, own_x, other_x, own_x_core, other_x_core, weight_ref, *rest):
    out_refs, (own_half, partner_half) = rest[:-2], rest[-2:]
    step = pl.program_id(0)
    height, wide = own_x.shape

    @pl.when(step == 0)
    def _():
        for target, mine, other in ((own_half, own_x, other_x), (partner_half, own_x_core, other_x_core)):
            target[pl.ds(pl.multiple_of(place[X] * height, height), height), :] = mine[...]
            target[pl.ds(pl.multiple_of((1 - place[X]) * height, height), height), :] = other[...]

    block = weight_ref.shape[1] // n_col
    columns = pl.ds(pl.multiple_of(order[step] * block, block), block)
    total = dot(own_half[...], weight_ref[pl.ds(pl.multiple_of(place[OWN] * wide, wide), wide), columns])
    total += dot(partner_half[...], weight_ref[pl.ds(pl.multiple_of(place[PARTNER] * wide, wide), wide), columns])
    value = total.astype(BF16)
    each = n_col // len(out_refs)
    for k, out_ref in enumerate(out_refs):
        @pl.when(step // each == k)
        def _(out_ref=out_ref):
            out_ref[...] = value


def whole(shape):
    return pl.BlockSpec(shape, lambda *_: (0,) * len(shape), pipeline_mode=pl.Buffered(1))


def params(limit):
    return pltpu.CompilerParams(dimension_semantics=("arbitrary",), vmem_limit_bytes=int(limit))


def cost(scale, flops, *sizes):
    return pl.CostEstimate(flops=int(flops * scale), bytes_accessed=int(sum(sizes) * scale), transcendentals=0)


def gate_up_call(place, tokens, rows, row_block, weights, n_col, which, split, scale, received=None):
    full, wide = weights[0].shape[0], weights[0].shape[1] // 2
    depth, half = full // n_col, rows // 2
    weight = pl.BlockSpec((depth, wide), lambda k, place: (place[BLOCKS + k], place[which]))
    token = pl.BlockSpec(
        (rows, tokens[0].shape[1]), lambda k, place: (row_block, 0), pipeline_mode=pl.Buffered(1)
    )
    in_specs = [token] * len(tokens) + [weight, weight]
    operands = [*tokens, *weights]
    shapes = [(w.stop - w.start, r.stop - r.start, wide) for w, r in pieces_of(rows, split)]
    if received is None:
        body, name = partner_kernel, "partner"
        out_shape, out_specs = [jax.ShapeDtypeStruct(a, BF16) for a in shapes], [whole(a) for a in shapes]
    else:
        body, name = own_kernel, "own"
        out_shape, out_specs = [jax.ShapeDtypeStruct((2, half, wide), BF16)] * 2, [whole((2, half, wide))] * 2
        in_specs += [whole(a) for a in shapes]
        operands += received
    return pl.pallas_call(
        functools.partial(body, len(tokens), split),
        out_shape=out_shape,
        grid_spec=pltpu.PrefetchScalarGridSpec(
            num_scalar_prefetch=1,
            grid=(n_col,),
            in_specs=in_specs,
            out_specs=out_specs,
            scratch_shapes=[pltpu.VMEM((n_col, rows, depth), BF16), pltpu.VMEM((2, rows, wide), F32)],
        ),
        compiler_params=params(GATE_UP_VMEM * MIB),
        cost_estimate=cost(scale, 4 * rows * full * wide, 4 * full * wide, 4 * rows * wide),
        name=name,
    )(place, *operands)


def down_call(place, order, pieces, down_weight, n_col, direct):
    half, wide = pieces[0].shape
    rows, block = 2 * half, down_weight.shape[1] // n_col
    if direct:
        out_shape = [jax.ShapeDtypeStruct((rows, block), BF16)] * n_col
        out_specs = [whole((rows, block))] * n_col
    else:
        out_shape = [jax.ShapeDtypeStruct((rows, 2 * block), BF16)] * 2
        out_specs = [
            pl.BlockSpec((rows, block), lambda d, place, order: (0, jnp.minimum(d, 1))),
            pl.BlockSpec((rows, block), lambda d, place, order: (0, jnp.maximum(d - 2, 0))),
        ]
    return pl.pallas_call(
        functools.partial(down_kernel, n_col, direct),
        out_shape=out_shape,
        grid_spec=pltpu.PrefetchScalarGridSpec(
            num_scalar_prefetch=2,
            grid=(n_col,),
            in_specs=[whole((half, wide))] * 4 + [pl.BlockSpec(memory_space=pltpu.VMEM)],
            out_specs=out_specs,
            scratch_shapes=[pltpu.VMEM((rows, wide), BF16)] * 2,
        ),
        compiler_params=params(DOWN_VMEM * MIB),
        cost_estimate=cost(DOWN_COST, 4 * rows * wide * block * n_col, 8 * half * wide),
        name="down",
    )(place, order, *pieces, down_weight)


def shifted(x, n, shift):
    return lax.ppermute(x, "col", [(i, (i + shift) % n) for i in range(n)])


def swapped(x, mask):
    return lax.ppermute(x, "row", [(i, i ^ mask) for i in range(4)])


def after(x, *deps):
    return lax.optimization_barrier((x,) + deps)[0]


def pipelined(tokens, gate_weight, up_weight, down_weight):
    n_col = 4
    eighth = tokens.shape[0] // 8
    weights = (gate_weight, up_weight)
    down_weight = pltpu.with_memory_space_constraint(down_weight, pltpu.VMEM)
    table = np.array(
        [
            [[1 - r % 2, r % 2, r // 2] + [(c - s) % n_col for s in range(n_col)] + [0]]
            + [[c ^ 1, c ^ 3, c, c ^ 2] * 2, [(c + 1) % n_col, (c + 2) % n_col, (c + 3) % n_col, c] * 2]
            for r in range(4)
            for c in range(n_col)
        ],
        np.int32,
    )
    mine = jnp.asarray(table)[lax.axis_index("row") * n_col + lax.axis_index("col")]
    place, halving, straight = mine[0], mine[1], mine[2]
    last = [place]

    def send_tokens(lo, hi):
        piece = after(tokens[lo * eighth : hi * eighth], *last)
        return [piece] + [shifted(piece, n_col, s) for s in range(1, n_col)]

    def scale(i, which):
        return FIRST_COST if i == 0 or (i, which) == (1, PARTNER) else GATE_UP_COST

    def partner(i):
        tok, rows, block = sources[i]
        out = gate_up_call(after(place, *last), tok, rows, block, weights, n_col, PARTNER, SPLIT[i], scale(i, PARTNER))
        last[:] = list(out)
        return [swapped(piece, 1) for piece in out]

    def own(i, received):
        tok, rows, block = sources[i]
        send, keep = gate_up_call(after(place, *last), tok, rows, block, weights, n_col, OWN, SPLIT[i], scale(i, OWN), received)
        last[:] = [send]
        return keep, swapped(send, 2)

    def gated(pair):
        keep, arrived = after(pair[0], *last), pair[1]
        gate = keep[0].astype(F32) + arrived[0].astype(F32)
        up = keep[1].astype(F32) + arrived[1].astype(F32)
        hidden = (jax.nn.silu(gate) * up).astype(BF16)
        last[:] = [hidden]
        return hidden, swapped(hidden, 2), swapped(hidden, 1)

    def relay(pieces):
        hidden, hidden_x, hidden_core = pieces
        return hidden, hidden_x, hidden_core, swapped(after(hidden_x, *last), 1)

    def down(pieces):
        send, keep = down_call(after(place, *last), halving, pieces, down_weight, n_col, False)
        last[:] = [send]
        return keep, lax.ppermute(send, "col", [(c, c ^ 1) for c in range(n_col)])

    def halve(pair):
        keep, arrived = after(pair[0], *last), pair[1]
        block = keep.shape[1] // 2
        total = [keep[:, at : at + block].astype(F32) + arrived[:, at : at + block].astype(F32) for at in (0, block)]
        send = total[1].astype(BF16)
        last[:] = [send]
        return total[0], lax.ppermute(send, "col", [(c, c ^ 2) for c in range(n_col)])

    def down_direct(pieces):
        out = down_call(after(place, *last), straight, pieces, down_weight, n_col, True)
        last[:] = out
        return [shifted(part, n_col, s + 1) for s, part in enumerate(out[:-1])] + [out[-1]]

    def sum_direct(out):
        total = after(out[-1], *last).astype(F32)
        for part in out[:-1]:
            total = total + part.astype(F32)
        out = total.astype(BF16)
        last[:] = [out]
        return out

    def finish(pair):
        out = (after(pair[0], *last) + pair[1].astype(F32)).astype(BF16)
        last[:] = [out]
        return out

    t0, t1 = send_tokens(0, 1), send_tokens(1, 3)
    sources = [(t0, eighth, 0), (t1, 2 * eighth, 0)]
    r0 = partner(0)
    t2 = send_tokens(3, 5)
    p0 = own(0, r0)
    r1 = partner(1)
    h0 = gated(p0)
    p1 = own(1, r1)
    t3 = send_tokens(5, 8)
    sources += [(t2, 2 * eighth, 0), (t3, 2 * eighth, 0), (t3, eighth, 2)]
    r2 = partner(2)
    h0 = relay(h0)
    d0 = down(h0)
    p2 = own(2, r2)
    h1 = gated(p1)
    r3 = partner(3)
    z0 = halve(d0)
    p3 = own(3, r3)
    h1 = relay(h1)
    h2 = gated(p2)
    r4 = partner(4)
    o0 = finish(z0)
    d1 = down(h1)
    p4 = own(4, r4)
    z1 = halve(d1)
    h2 = relay(h2)
    h3 = gated(p3)
    d2 = down(h2)
    o1 = finish(z1)
    h3 = relay(h3)
    h4 = gated(p4)
    z2 = halve(d2)
    d3 = down(h3)
    h4 = relay(h4)
    o2 = finish(z2)
    d4 = down_direct(h4)
    z3 = halve(d3)
    o4 = sum_direct(d4)
    o3 = finish(z3)
    return jnp.concatenate([o0, o1, o2, o3, o4], axis=0)


def generic(tokens, gate_weight, up_weight, down_weight):
    gathered = lax.all_gather(tokens, "col", axis=1, tiled=True)
    gate = lax.psum_scatter(dot(gathered, gate_weight).astype(BF16), "row", scatter_dimension=0, tiled=True)
    up = lax.psum_scatter(dot(gathered, up_weight).astype(BF16), "row", scatter_dimension=0, tiled=True)
    hidden = (jax.nn.silu(gate.astype(F32)) * up.astype(F32)).astype(BF16)
    hidden = lax.all_gather(hidden, "row", axis=0, tiled=True)
    partial = dot(hidden, down_weight).astype(BF16)
    return lax.psum_scatter(partial, "col", scatter_dimension=1, tiled=True)


def solution(mesh):
    n_row, n_col = mesh.shape["row"], mesh.shape["col"]
    in_specs = (P("groups", ("row", "col")), P("row", "col"), P("row", "col"), P("col", "row"))
    out_specs = P("groups", ("row", "col"))
    step = pipelined if (n_row, n_col) == (4, 4) else generic
    return jax.shard_map(step, mesh=mesh, in_specs=in_specs, out_specs=out_specs, check_vma=False)
```

```python
import functools

import jax
import jax.numpy as jnp
import numpy as np
from jax import lax
from jax.experimental import pallas as pl
from jax.experimental.pallas import tpu as pltpu
from jax.sharding import PartitionSpec as P

BF16, F32 = jnp.bfloat16, jnp.float32
FIRST_COST, GATE_UP_COST, DOWN_COST = 1, 0.2, 0.2
SPLIT = (4, 4, 4, 4, 1)
MIB, GATE_UP_VMEM, DOWN_VMEM = 2**20, 29, 29
PARTNER, OWN, X, BLOCKS = 0, 1, 2, 3


def dot(a, b):
    return jnp.dot(a, b, preferred_element_type=F32)


def accumulate(place, token_refs, gate_ref, up_ref, stage, acc):
    step, depth = pl.program_id(0), gate_ref.shape[0]

    @pl.when(step == 0)
    def _():
        acc[...] = jnp.zeros_like(acc)
        for k in range(stage.shape[0]):
            if len(token_refs) == 1:
                stage[k] = token_refs[0][:, k * depth : (k + 1) * depth]
            else:
                stage[k] = token_refs[k][...]

    tok = stage[step]
    acc[0] += dot(tok, gate_ref[...])
    acc[1] += dot(tok, up_ref[...])


def pieces_of(rows, split):
    if split == 1:
        return [(slice(0, 2), slice(0, rows))]
    height = 2 * rows // split
    return [(slice(w, w + 1), slice(at, at + height)) for w in (0, 1) for at in range(0, rows, height)]


def partner_kernel(n_tok, split, place, *refs):
    token_refs, (gate_ref, up_ref, *out_refs), (stage, acc) = refs[:n_tok], refs[n_tok:-2], refs[-2:]
    accumulate(place, token_refs, gate_ref, up_ref, stage, acc)

    @pl.when(pl.program_id(0) == pl.num_programs(0) - 1)
    def _():
        for (which, rows), out_ref in zip(pieces_of(acc.shape[1], split), out_refs):
            out_ref[...] = acc[which, rows].astype(BF16)


def own_kernel(n_tok, split, place, *refs):
    token_refs, (gate_ref, up_ref, *received_refs) = refs[:n_tok], refs[n_tok:-4]
    send_ref, keep_ref, stage, acc = refs[-4:]
    accumulate(place, token_refs, gate_ref, up_ref, stage, acc)
    half = send_ref.shape[1]

    @pl.when(pl.program_id(0) == pl.num_programs(0) - 1)
    def _():
        for (which, rows), ref in zip(pieces_of(acc.shape[1], split), received_refs):
            acc[which, rows] += ref[...].astype(F32)
        for ref, x in ((send_ref, 1 - place[X]), (keep_ref, place[X])):
            ref[...] = acc[:, pl.ds(pl.multiple_of(x * half, half), half), :].astype(BF16)


def down_kernel(n_col, direct, place, order, own_x, other_x, own_x_core, other_x_core, weight_ref, *rest):
    out_refs, (own_half, partner_half) = rest[:-2], rest[-2:]
    step = pl.program_id(0)
    height, wide = own_x.shape

    @pl.when(step == 0)
    def _():
        for target, mine, other in ((own_half, own_x, other_x), (partner_half, own_x_core, other_x_core)):
            target[pl.ds(pl.multiple_of(place[X] * height, height), height), :] = mine[...]
            target[pl.ds(pl.multiple_of((1 - place[X]) * height, height), height), :] = other[...]

    block = weight_ref.shape[1] // n_col
    columns = pl.ds(pl.multiple_of(order[step] * block, block), block)
    total = dot(own_half[...], weight_ref[pl.ds(pl.multiple_of(place[OWN] * wide, wide), wide), columns])
    total += dot(partner_half[...], weight_ref[pl.ds(pl.multiple_of(place[PARTNER] * wide, wide), wide), columns])
    value = total.astype(BF16)
    each = n_col // len(out_refs)
    for k, out_ref in enumerate(out_refs):
        @pl.when(step // each == k)
        def _(out_ref=out_ref):
            out_ref[...] = value


def whole(shape):
    return pl.BlockSpec(shape, lambda *_: (0,) * len(shape), pipeline_mode=pl.Buffered(1))


def params(limit):
    return pltpu.CompilerParams(dimension_semantics=("arbitrary",), vmem_limit_bytes=int(limit))


def cost(scale, flops, *sizes):
    return pl.CostEstimate(flops=int(flops * scale), bytes_accessed=int(sum(sizes) * scale), transcendentals=0)


def gate_up_call(place, tokens, rows, row_block, weights, n_col, which, split, scale, received=None):
    full, wide = weights[0].shape[0], weights[0].shape[1] // 2
    depth, half = full // n_col, rows // 2
    weight = pl.BlockSpec((depth, wide), lambda k, place: (place[BLOCKS + k], place[which]))
    token = pl.BlockSpec(
        (rows, tokens[0].shape[1]), lambda k, place: (row_block, 0), pipeline_mode=pl.Buffered(1)
    )
    in_specs = [token] * len(tokens) + [weight, weight]
    operands = [*tokens, *weights]
    shapes = [(w.stop - w.start, r.stop - r.start, wide) for w, r in pieces_of(rows, split)]
    if received is None:
        body, name = partner_kernel, "partner"
        out_shape, out_specs = [jax.ShapeDtypeStruct(a, BF16) for a in shapes], [whole(a) for a in shapes]
    else:
        body, name = own_kernel, "own"
        out_shape, out_specs = [jax.ShapeDtypeStruct((2, half, wide), BF16)] * 2, [whole((2, half, wide))] * 2
        in_specs += [whole(a) for a in shapes]
        operands += received
    return pl.pallas_call(
        functools.partial(body, len(tokens), split),
        out_shape=out_shape,
        grid_spec=pltpu.PrefetchScalarGridSpec(
            num_scalar_prefetch=1,
            grid=(n_col,),
            in_specs=in_specs,
            out_specs=out_specs,
            scratch_shapes=[pltpu.VMEM((n_col, rows, depth), BF16), pltpu.VMEM((2, rows, wide), F32)],
        ),
        compiler_params=params(GATE_UP_VMEM * MIB),
        cost_estimate=cost(scale, 4 * rows * full * wide, 4 * full * wide, 4 * rows * wide),
        name=name,
    )(place, *operands)


def down_call(place, order, pieces, down_weight, n_col, direct):
    half, wide = pieces[0].shape
    rows, block = 2 * half, down_weight.shape[1] // n_col
    if direct:
        out_shape = [jax.ShapeDtypeStruct((rows, block), BF16)] * n_col
        out_specs = [whole((rows, block))] * n_col
    else:
        out_shape = [jax.ShapeDtypeStruct((rows, 2 * block), BF16)] * 2
        out_specs = [
            pl.BlockSpec((rows, block), lambda d, place, order: (0, jnp.minimum(d, 1))),
            pl.BlockSpec((rows, block), lambda d, place, order: (0, jnp.maximum(d - 2, 0))),
        ]
    return pl.pallas_call(
        functools.partial(down_kernel, n_col, direct),
        out_shape=out_shape,
        grid_spec=pltpu.PrefetchScalarGridSpec(
            num_scalar_prefetch=2,
            grid=(n_col,),
            in_specs=[whole((half, wide))] * 4 + [pl.BlockSpec(memory_space=pltpu.VMEM)],
            out_specs=out_specs,
            scratch_shapes=[pltpu.VMEM((rows, wide), BF16)] * 2,
        ),
        compiler_params=params(DOWN_VMEM * MIB),
        cost_estimate=cost(DOWN_COST, 4 * rows * wide * block * n_col, 8 * half * wide),
        name="down",
    )(place, order, *pieces, down_weight)


def shifted(x, n, shift):
    return lax.ppermute(x, "col", [(i, (i + shift) % n) for i in range(n)])


def swapped(x, mask):
    return lax.ppermute(x, "row", [(i, i ^ mask) for i in range(4)])


def after(x, *deps):
    return lax.optimization_barrier((x,) + deps)[0]


def pipelined(tokens, gate_weight, up_weight, down_weight):
    n_col = 4
    eighth = tokens.shape[0] // 8
    weights = (gate_weight, up_weight)
    down_weight = pltpu.with_memory_space_constraint(down_weight, pltpu.VMEM)
    table = np.array(
        [
            [[1 - r % 2, r % 2, r // 2] + [(c - s) % n_col for s in range(n_col)] + [0]]
            + [[c ^ 1, c ^ 3, c, c ^ 2] * 2, [(c + 1) % n_col, (c + 2) % n_col, (c + 3) % n_col, c] * 2]
            for r in range(4)
            for c in range(n_col)
        ],
        np.int32,
    )
    mine = jnp.asarray(table)[lax.axis_index("row") * n_col + lax.axis_index("col")]
    place, halving, straight = mine[0], mine[1], mine[2]
    last = [place]

    def send_tokens(lo, hi):
        piece = after(tokens[lo * eighth : hi * eighth], *last)
        return [piece] + [shifted(piece, n_col, s) for s in range(1, n_col)]

    def scale(i, which):
        return FIRST_COST if i == 0 or (i, which) == (1, PARTNER) else GATE_UP_COST

    def partner(i):
        tok, rows, block = sources[i]
        out = gate_up_call(after(place, *last), tok, rows, block, weights, n_col, PARTNER, SPLIT[i], scale(i, PARTNER))
        last[:] = list(out)
        return [swapped(piece, 1) for piece in out]

    def own(i, received):
        tok, rows, block = sources[i]
        send, keep = gate_up_call(after(place, *last), tok, rows, block, weights, n_col, OWN, SPLIT[i], scale(i, OWN), received)
        last[:] = [send]
        return keep, swapped(send, 2)

    def gated(pair):
        keep, arrived = after(pair[0], *last), pair[1]
        gate = keep[0].astype(F32) + arrived[0].astype(F32)
        up = keep[1].astype(F32) + arrived[1].astype(F32)
        hidden = (jax.nn.silu(gate) * up).astype(BF16)
        last[:] = [hidden]
        return hidden, swapped(hidden, 2), swapped(hidden, 1)

    def relay(pieces):
        hidden, hidden_x, hidden_core = pieces
        return hidden, hidden_x, hidden_core, swapped(after(hidden_x, *last), 1)

    def down(pieces):
        send, keep = down_call(after(place, *last), halving, pieces, down_weight, n_col, False)
        last[:] = [send]
        return keep, lax.ppermute(send, "col", [(c, c ^ 1) for c in range(n_col)])

    def halve(pair):
        keep, arrived = after(pair[0], *last), pair[1]
        block = keep.shape[1] // 2
        total = [keep[:, at : at + block].astype(F32) + arrived[:, at : at + block].astype(F32) for at in (0, block)]
        send = total[1].astype(BF16)
        last[:] = [send]
        return total[0], lax.ppermute(send, "col", [(c, c ^ 2) for c in range(n_col)])

    def down_direct(pieces):
        out = down_call(after(place, *last), straight, pieces, down_weight, n_col, True)
        last[:] = out
        return [shifted(part, n_col, s + 1) for s, part in enumerate(out[:-1])] + [out[-1]]

    def sum_direct(out):
        total = after(out[-1], *last).astype(F32)
        for part in out[:-1]:
            total = total + part.astype(F32)
        out = total.astype(BF16)
        last[:] = [out]
        return out

    def finish(pair):
        out = (after(pair[0], *last) + pair[1].astype(F32)).astype(BF16)
        last[:] = [out]
        return out

    t0, t1 = send_tokens(0, 1), send_tokens(1, 3)
    sources = [(t0, eighth, 0), (t1, 2 * eighth, 0)]
    r0 = partner(0)
    t2 = send_tokens(3, 5)
    p0 = own(0, r0)
    r1 = partner(1)
    h0 = gated(p0)
    p1 = own(1, r1)
    t3 = send_tokens(5, 8)
    sources += [(t2, 2 * eighth, 0), (t3, 2 * eighth, 0), (t3, eighth, 2)]
    r2 = partner(2)
    h0 = relay(h0)
    d0 = down(h0)
    p2 = own(2, r2)
    h1 = gated(p1)
    r3 = partner(3)
    z0 = halve(d0)
    p3 = own(3, r3)
    h1 = relay(h1)
    h2 = gated(p2)
    r4 = partner(4)
    o0 = finish(z0)
    d1 = down(h1)
    p4 = own(4, r4)
    z1 = halve(d1)
    h2 = relay(h2)
    h3 = gated(p3)
    d2 = down(h2)
    h3 = relay(h3)
    d3 = down(h3)
    h4 = gated(p4)
    o1 = finish(z1)
    z2 = halve(d2)
    h4 = relay(h4)
    z3 = halve(d3)
    o2 = finish(z2)
    d4 = down_direct(h4)
    o4 = sum_direct(d4)
    o3 = finish(z3)
    return jnp.concatenate([o0, o1, o2, o3, o4], axis=0)


def generic(tokens, gate_weight, up_weight, down_weight):
    gathered = lax.all_gather(tokens, "col", axis=1, tiled=True)
    gate = lax.psum_scatter(dot(gathered, gate_weight).astype(BF16), "row", scatter_dimension=0, tiled=True)
    up = lax.psum_scatter(dot(gathered, up_weight).astype(BF16), "row", scatter_dimension=0, tiled=True)
    hidden = (jax.nn.silu(gate.astype(F32)) * up.astype(F32)).astype(BF16)
    hidden = lax.all_gather(hidden, "row", axis=0, tiled=True)
    partial = dot(hidden, down_weight).astype(BF16)
    return lax.psum_scatter(partial, "col", scatter_dimension=1, tiled=True)


def solution(mesh):
    n_row, n_col = mesh.shape["row"], mesh.shape["col"]
    in_specs = (P("groups", ("row", "col")), P("row", "col"), P("row", "col"), P("col", "row"))
    out_specs = P("groups", ("row", "col"))
    step = pipelined if (n_row, n_col) == (4, 4) else generic
    return jax.shard_map(step, mesh=mesh, in_specs=in_specs, out_specs=out_specs, check_vma=False)
```
